512 devices in a mesh: cuts: 4 (over y_hi, core), mode: 128 (over x, y_lo, z).
Axes of the slice: x: 4, y: 8 (y_hi: 2, y_lo: 4; y = y_hi * 4 + y_lo), z: 8, core: 2. Of those that a mesh axis runs over, the one named last changes fastest.
Arguments:
- stem: bfloat16 [4, 2, 1024, 16384], P('cuts', None, None, 'mode'), may hold values from -6 to 6
- branches: bfloat16 [3, 2, 1024, 1024], P(None, None, None, 'mode'), may hold values from -0.125 to 0.125
- order: int32 [3], replicated, may hold values from 0 to 2, each once
- swap_order: int32 [3, 1024], replicated, may hold values from 0 to 1023, each once within a row
- row_bits: int32 [2048], replicated, may hold values from 0 to 1023
- column_bits: int32 [2048], replicated, may hold values from 0 to 16383
Outputs:
- stem_out: bfloat16 [4, 2, 1024, 16384], P('cuts', None, None, 'mode')
- amplitudes: float32 [2, 2048], P(None, ('cuts', 'mode'))
The draws below stay inside these ranges and needn't reach their ends.
All inputs are finite; a program needn't handle non-finite values.
Results may differ from the reference program's by a relative error of at most 0.009.
Values may be sent and summed in bfloat16 or wider, within the bound.
A program may use at most 128 MiB of HBM per device.

```python
import jax
import jax.numpy as jnp
from jax import lax

K = 1024
STEPS = 3
NB = 2048
SLICES = 4
COLS = 16384
N_MODE = 128


def touch_ends(array, rng, smallest, high):
    longest = array.shape.index(max(array.shape))
    spots = []
    for shift in (0, 1):
        where = [jax.random.randint(jax.random.fold_in(rng, axis), (), 0, length) for axis, length in enumerate(array.shape)]
        where[longest] = (where[longest] + shift) % array.shape[longest]
        spots.append(tuple(where))
    return array.at[spots[0]].set(smallest).at[spots[1]].set(high)


def levels(key, shape, cuts, smallest, largest):
    factor_of, own = 1.0, jax.random.fold_in(key, 6)
    for dim, shards_of in cuts:
        draws = jnp.exp(jax.random.uniform(jax.random.fold_in(own, dim), (shards_of,), jnp.float32, smallest / len(cuts), largest / len(cuts)))
        factor_of = factor_of * jnp.repeat(draws, shape[dim] // shards_of).reshape([-1 if axis == dim else 1 for axis in range(len(shape))])
    return factor_of


def gaussian(key, dims, scale, bound, cuts=(), held_as=jnp.bfloat16):
    array = jax.random.normal(key, dims, jnp.float32) * scale
    if len(cuts) > 0:
        array = levels(key, dims, cuts, -0.22, 0.18) * array
    return jnp.clip(array, min=-bound, max=bound).astype(held_as)


def setup_inputs(seed: int = 0) -> dict:
    key_list = jax.random.split(jax.random.key(seed), 7)
    stem = gaussian(key_list[0], (SLICES, 2, K, COLS), 1.0, 6.0, ((0, 4), (3, 128)))
    branches = gaussian(key_list[1], (STEPS, 2, K, K), (2 * K) ** -0.5, 0.125, ((3, 128),))
    order = jax.random.permutation(key_list[2], STEPS).astype(jnp.int32)
    swap_order = jax.vmap(lambda own: jax.random.permutation(own, K))(jax.random.split(key_list[3], STEPS)).reshape((STEPS, K)).astype(jnp.int32)
    row_bits = touch_ends(jax.random.randint(key_list[4], (NB,), 0, K), jax.random.fold_in(key_list[4], 1), 0, K - 1).astype(jnp.int32)
    column_bits = touch_ends(jax.random.randint(key_list[5], (NB,), 0, COLS), jax.random.fold_in(key_list[5], 1), 0, COLS - 1).astype(jnp.int32)
    return {"stem": stem, "branches": branches, "order": order, "swap_order": swap_order, "row_bits": row_bits, "column_bits": column_bits}


def swap_modes(field, groups):
    slices, two, width, cols = field.shape
    rows = cols // groups
    view = field.reshape(slices, two, groups, width // groups, groups, rows)
    view = view.transpose(0, 1, 4, 3, 2, 5)
    return view.reshape(slices, two, width, cols)


def absorb_slice(matrix, part):
    first = matrix[0]
    second = matrix[1]
    xreal = part[0].astype(jnp.float32)
    ximag = part[1].astype(jnp.float32)
    hp = lax.Precision.HIGHEST
    real = jnp.einsum("io,ic->oc", first, xreal, precision=hp) - jnp.einsum("io,ic->oc", second, ximag, precision=hp)
    imag = jnp.einsum("io,ic->oc", first, ximag, precision=hp) + jnp.einsum("io,ic->oc", second, xreal, precision=hp)
    return jnp.stack([real, imag], axis=0).astype(jnp.bfloat16)


def reference(stem, branches, order, swap_order, row_bits, column_bits):
    field = stem
    for step in range(STEPS):
        field = jnp.take(field, swap_order[step].astype(jnp.int32), axis=2)
        field = swap_modes(field, N_MODE)
        matrix = lax.dynamic_index_in_dim(branches, order[step].astype(jnp.int32), 0, keepdims=False).astype(jnp.float32)
        field = lax.map(lambda part: absorb_slice(matrix, part), field)
    picked = field[:, :, row_bits, column_bits].astype(jnp.float32)
    amplitudes = jnp.sum(picked, axis=0)
    return field, amplitudes
```

```python
import functools

import jax
import jax.numpy as jnp
from jax import lax
from jax.experimental import pallas as pl
from jax.experimental.pallas import tpu as pltpu
from jax.sharding import PartitionSpec as P

MESH = pl.DeviceIdType.MESH
BF = jnp.bfloat16
F32 = jnp.float32
SIZE = {"x": 4, "y": 4, "z": 8}
ORDERS = ("xyz", "yzx", "zxy")
LANES = (
    ((0, 256), (256, 128), (384, 128)),
    ((0, 128), (128, 256), (384, 128)),
    ((0, 128), (128, 128), (256, 256)),
)
LAG = 2


def kernel(order, stem, br, idx, rb, cb, out, amp, MT, Y, X, S, Y3T, snd1, rcv1, snd2, rcv2, a0, a1, a2, a3, a4,
           s_a2a, r_a2a, s_ag, r_ag, s_p, r_p, s_am, r_am):
    c = lax.axis_index("cuts")
    m = lax.axis_index("mode")
    core, yh = c % 2, c // 2
    me = {"x": m // 32, "y": (m // 8) % 4, "z": m % 8}
    yg = yh * 4 + me["y"]

    def mode_of(x, y, z):
        return x * 32 + y * 8 + z

    def near(d, step):
        if d == "x":
            return c, mode_of((me["x"] + step + 4) % 4, me["y"], me["z"])
        if d == "z":
            return c, mode_of(me["x"], me["y"], (me["z"] + step + 8) % 8)
        g = (yg + step + 8) % 8
        return (g // 4) * 2 + core, mode_of(me["x"], g % 4, me["z"])

    def far(i):
        k = (i * 37) % 128
        return mode_of((me["x"] + k // 32) % 4, (me["y"] + (k // 8) % 4) % 4, (me["z"] + k % 8) % 8)

    barrier = pltpu.get_barrier_semaphore()

    def greet(i, carry):
        pl.semaphore_signal(barrier, inc=1, device_id=(c, far(i)), device_id_type=MESH)
        return carry

    lax.fori_loop(1, 128, greet, 0)
    for k in range(1, 4):
        pl.semaphore_signal(barrier, inc=1, device_id=((c + k) % 4, m), device_id_type=MESH)
    for k in (-1, 1):
        pl.semaphore_signal(barrier, inc=1, device_id=near("y", k), device_id_type=MESH)

    for t in range(3):
        mine = br[order[t]]
        MT[t, core, me["x"], me["y"], me["z"]] = jnp.where(core == 0, mine[:, :512], mine[:, 512:])

    lane = lax.broadcasted_iota(jnp.int32, (128, 1024), 1)

    def permute(t, put):
        for k in range(8):
            hot = (lane == idx[t, :, k : k + 1]).astype(F32).astype(BF)
            z = jnp.dot(hot, Y[...], preferred_element_type=F32)
            put(k, 0, z[:, :128].T)
            put(k, 1, z[:, 128:].T)

    Y[:, :128] = stem[0]
    Y[:, 128:] = stem[1]

    def put_send(k, p, block):
        S[pl.ds(p * 8 + k, 128, stride=16), :] = block

    permute(0, put_send)
    snd1[...] = S[...].reshape(128, 16, 128).astype(BF)
    pl.semaphore_wait(barrier, 132)

    def exchange(send, recv, n):
        def go(i, carry):
            peer = far(i)
            pltpu.make_async_remote_copy(
                src_ref=send.at[peer], dst_ref=recv.at[m], send_sem=s_a2a.at[n], recv_sem=r_a2a.at[n],
                device_id=(c, peer), device_id_type=MESH,
            ).start()
            return carry

        lax.fori_loop(1, 128, go, 0)
        recv[m] = send[m]

    def exchange_wait(send, recv, n):
        copy = pltpu.make_async_remote_copy(
            src_ref=send.at[pl.ds(0, 127)], dst_ref=recv.at[pl.ds(0, 127)], send_sem=s_a2a.at[n], recv_sem=r_a2a.at[n],
            device_id=(c, far(1)), device_id_type=MESH,
        )
        copy.wait_send()
        copy.wait_recv()

    partner = (yh * 2 + 1 - core, m)

    def share(t, region):
        pltpu.make_async_remote_copy(
            src_ref=region, dst_ref=region, send_sem=s_p.at[t], recv_sem=r_p.at[t], device_id=partner, device_id_type=MESH
        ).start()

    def gather_steps(t, kind):
        start, width = LANES[t][kind]
        item = t * 3 + kind
        dims = ORDERS[kind]
        steps = []
        count = [0]
        waiting = []
        sent = []

        def region(ph, q, half=None):
            at = []
            for d in "xyz":
                place = dims.index(d)
                if place < ph:
                    if half is not None and place == ph - 1:
                        at.append(pl.ds(half * (SIZE[d] // 2), SIZE[d] // 2))
                    else:
                        at.append(pl.ds(0, SIZE[d]))
                elif place == ph:
                    at.append(q)
                else:
                    at.append(me[d])
            return MT.at[t, core, at[0], at[1], at[2], :, pl.ds(start, width)]

        def hop(d, step, src, landing):
            k = count[0]
            count[0] += 1
            copy = pltpu.make_async_remote_copy(
                src_ref=src, dst_ref=src, send_sem=s_ag.at[item, k], recv_sem=r_ag.at[item, k],
                device_id=near(d, step), device_id_type=MESH,
            )
            arrive = pltpu.make_async_remote_copy(
                src_ref=landing, dst_ref=landing, send_sem=s_ag.at[item, k], recv_sem=r_ag.at[item, k],
                device_id=near(d, step), device_id_type=MESH,
            )
            copy.start()
            sent.append(copy)
            waiting.append((arrive, landing))

        def settle(last):
            for arrive, landing in waiting:
                arrive.wait_recv()
                if last:
                    share(t, landing)
            waiting.clear()

        def make(ph, s):
            d = dims[ph]
            n = SIZE[d]
            q = me[d]
            top = n // 2 - 1

            def at(k):
                return (q + k + n) % n

            def step():
                settle(ph == 2 and s > 0)
                if ph == 2 and s == 0:
                    share(t, region(2, q))
                if s < top:
                    hop(d, 1, region(ph, at(-s)), region(ph, at(-s - 1)))
                    hop(d, -1, region(ph, at(s)), region(ph, at(s + 1)))
                elif ph == 0:
                    hop(d, 1, region(ph, at(-s)), region(ph, at(-s - 1)))
                else:
                    hop(d, 1, region(ph, at(-s), 0), region(ph, at(-s - 1), 0))
                    hop(d, -1, region(ph, at(s), 1), region(ph, at(s + 1), 1))

            return step

        for ph in range(3):
            for s in range(SIZE[dims[ph]] // 2):
                steps.append(make(ph, s))
        steps.append(lambda: settle(True))

        def finish():
            for copy in sent:
                copy.wait_send()

        return steps, finish

    items = [[gather_steps(t, kind) for kind in range(3)] for t in range(3)]
    n_steps = len(items[0][0][0])

    exchange(snd1, rcv1, 0)
    for turn in range(n_steps + 2 * LAG):
        for t in range(3):
            s = turn - t * LAG
            if 0 <= s < n_steps:
                for kind in range(3):
                    items[t][kind][0][s]()

    def share_wait(t):
        copy = pltpu.make_async_remote_copy(
            src_ref=MT.at[t, core], dst_ref=MT.at[t, 1 - core], send_sem=s_p.at[t], recv_sem=r_p.at[t],
            device_id=partner, device_id_type=MESH,
        )
        copy.wait_send()
        copy.wait_recv()

    def absorb(t):
        def part(g, carry):
            gx, gy = g // 2, g % 2
            low = MT[t, 0, gx, pl.ds(gy * 2, 2)].reshape(256, 512)
            high = MT[t, 1, gx, pl.ds(gy * 2, 2)].reshape(256, 512)
            o = jnp.dot(low, X[:512], preferred_element_type=F32) + jnp.dot(high, X[512:], preferred_element_type=F32)
            o = o.reshape(16, 16, 256)
            re = o[:, :8, :128] - o[:, 8:, 128:]
            im = o[:, :8, 128:] + o[:, 8:, :128]
            rows = pl.ds(pl.multiple_of(g * 128, 128), 128)
            Y[rows, :128] = re.reshape(128, 128).astype(BF)
            Y[rows, 128:] = im.reshape(128, 128).astype(BF)
            return carry

        lax.fori_loop(0, 8, part, 0)

    exchange_wait(snd1, rcv1, 0)
    first = rcv1[...].astype(F32)
    X[:, :128] = first[:, :8, :].reshape(1024, 128).astype(BF)
    X[:, 128:] = first[:, 8:, :].reshape(1024, 128).astype(BF)

    def put_next(k, p, block):
        S[pl.ds(p * 1024 + k, 128, stride=8), :] = block

    for t in range(3):
        if t > 0:
            permute(t, put_next)
            X[:, :128] = S[:1024].astype(BF)
            X[:, 128:] = S[1024:].astype(BF)
        share_wait(t)
        absorb(t)

    for p in range(2):
        for j in range(8):
            block = Y[j * 128 : (j + 1) * 128, p * 128 : (p + 1) * 128].astype(F32).T
            S[pl.ds(p * 8 + j, 128, stride=16), :] = block
            Y3T[p * 128 : (p + 1) * 128, j * 128 : (j + 1) * 128] = block.astype(BF)
    snd2[...] = S[...].reshape(128, 16, 128).astype(BF)
    exchange(snd2, rcv2, 1)

    state = lax.broadcasted_iota(jnp.int32, (1024, 512), 0)
    place = lax.broadcasted_iota(jnp.int32, (128, 512), 0)
    for q in range(4):
        rows = rb[:, q * 512 : (q + 1) * 512]
        cols = cb[:, q * 512 : (q + 1) * 512]
        hot = (state == rows).astype(F32).astype(BF)
        got = jnp.dot(Y3T[...], hot, preferred_element_type=F32)
        here = (place == cols // 128) & (cols % 128 == m)
        for p in range(2):
            val = jnp.sum(jnp.where(here, got[p * 128 : (p + 1) * 128], 0.0), axis=0, keepdims=True)
            a0[q, p : p + 1, :] = val

    def spread(src_of, buf, peers, mine, n):
        copies = []
        for k, peer in enumerate(peers):
            copy = pltpu.make_async_remote_copy(
                src_ref=src_of(k), dst_ref=buf.at[k + 1], send_sem=s_am.at[n, k], recv_sem=r_am.at[n, k],
                device_id=peer, device_id_type=MESH,
            )
            copy.start()
            copies.append(copy)
        buf[0] = mine
        for copy in copies:
            copy.wait()
        total = buf[0]
        for k in range(len(peers)):
            total = total + buf[k + 1]
        return total

    t1 = spread(lambda k: a0.at[(c + k + 1) % 4], a1, [((c + k) % 4, m) for k in range(1, 4)], a0[c], 0)
    for g in range(4):
        a2[g, :, :] = t1[:, g * 128 : (g + 1) * 128]
    mx = me["x"]
    t2 = spread(
        lambda k: a2.at[(mx + k + 1) % 4], a3,
        [(c, mode_of((mx + k) % 4, me["y"], me["z"])) for k in range(1, 4)], a2[mx], 1,
    )
    a2[4] = t2
    t3 = spread(
        lambda k: a2.at[4], a3.at[pl.ds(4, 4)],
        [(c, mode_of(mx, (me["y"] + k) % 4, me["z"])) for k in range(1, 4)], t2, 2,
    )
    a2[5] = t3
    t4 = spread(
        lambda k: a2.at[5], a4,
        [(c, mode_of(mx, me["y"], (me["z"] + k) % 8)) for k in range(1, 8)], t3, 3,
    )
    amp[...] = t4

    for t in range(3):
        for kind in range(3):
            items[t][kind][1]()
    exchange_wait(snd2, rcv2, 1)
    S[...] = rcv2[...].astype(F32).reshape(2048, 128)
    for p in range(2):
        for j in range(8):
            block = S[pl.ds(p * 8 + j, 128, stride=16), :]
            out[p, j * 128 : (j + 1) * 128, :] = block.T.astype(BF)


def body(stem, branches, order, swap_order, row_bits, column_bits):
    vmem = pl.BlockSpec(memory_space=pltpu.VMEM)
    br = branches.transpose(0, 1, 3, 2).reshape(3, 16, 1024)
    idx = swap_order.reshape(3, 128, 8)
    dma = pltpu.SemaphoreType.DMA
    field, amps = pl.pallas_call(
        kernel,
        out_shape=(jax.ShapeDtypeStruct((2, 1024, 128), BF), jax.ShapeDtypeStruct((2, 128), F32)),
        in_specs=[pl.BlockSpec(memory_space=pltpu.SMEM)] + [vmem] * 5,
        out_specs=(vmem, vmem),
        scratch_shapes=[
            pltpu.VMEM((3, 2, 4, 4, 8, 16, 512), BF),
            pltpu.VMEM((1024, 256), BF),
            pltpu.VMEM((1024, 256), BF),
            pltpu.VMEM((2048, 128), F32),
            pltpu.VMEM((256, 1024), BF),
            pltpu.VMEM((128, 16, 128), BF),
            pltpu.VMEM((128, 16, 128), BF),
            pltpu.VMEM((128, 16, 128), BF),
            pltpu.VMEM((128, 16, 128), BF),
            pltpu.VMEM((4, 2, 512), F32),
            pltpu.VMEM((4, 2, 512), F32),
            pltpu.VMEM((6, 2, 128), F32),
            pltpu.VMEM((8, 2, 128), F32),
            pltpu.VMEM((8, 2, 128), F32),
            dma((2,)), dma((2,)),
            dma((9, 16)), dma((9, 16)),
            dma((3,)), dma((3,)),
            dma((4, 7)), dma((4, 7)),
        ],
        compiler_params=pltpu.CompilerParams(collective_id=0, has_side_effects=True, vmem_limit_bytes=48 * 1024 * 1024),
    )(order, stem[0], br, idx, row_bits.reshape(1, 2048), column_bits.reshape(1, 2048))
    m = lax.axis_index("mode")
    amps = lax.dynamic_slice_in_dim(amps, (m % 32) * 4, 4, 1)
    return field[None], amps


def solution(mesh):
    placed = (P("cuts", None, None, "mode"), P(None, None, None, "mode"), P(), P(), P(), P())
    return jax.shard_map(
        body,
        mesh=mesh,
        in_specs=placed,
        out_specs=(P("cuts", None, None, "mode"), P(None, ("cuts", "mode"))),
        check_vma=False,
    )
```

```python
import functools

import jax
import jax.numpy as jnp
from jax import lax
from jax.experimental import pallas as pl
from jax.experimental.pallas import tpu as pltpu
from jax.sharding import PartitionSpec as P

MESH = pl.DeviceIdType.MESH
BF = jnp.bfloat16
F32 = jnp.float32
SIZE = {"x": 4, "y": 4, "z": 8}
ORDERS = ("xyz", "zyx", "zxy")
DIRECT = ((0, 1), (0,), (0,))
HALF = (("", "", "x"), ("", "z", "y"), ("", "z", "x"))
TILES = (((0, 2), (2, 1)), ((0, 1), (1, 2)), ((0, 2), (2, 1)))
LAG = 0


def kernel(order, stem_h, br_h, idx, rb, cb, out, amp, stem, br, MA, MB, Y, X, S, Y3T, snd1, rcv1, snd2, rcv2, a0, a1, a2, a3, a4,
           s_a2a, r_a2a, s_ag, r_ag, s_p, r_p, s_am, r_am, s_in, plane, cube):
    c = lax.axis_index("cuts")
    m = lax.axis_index("mode")
    core, yh = c % 2, c // 2
    me = {"x": m // 32, "y": (m // 8) % 4, "z": m % 8}
    yg = yh * 4 + me["y"]

    def mode_of(x, y, z):
        return x * 32 + y * 8 + z

    def near(d, step):
        if d == "x":
            return c, mode_of((me["x"] + step + 4) % 4, me["y"], me["z"])
        if d == "z":
            return c, mode_of(me["x"], me["y"], (me["z"] + step + 8) % 8)
        g = (yg + step + 8) % 8
        return (g // 4) * 2 + core, mode_of(me["x"], g % 4, me["z"])

    def far(i):
        k = (i * 37) % 128
        return mode_of((me["x"] + k // 32) % 4, (me["y"] + (k // 8) % 4) % 4, (me["z"] + k % 8) % 8)

    get_stem = pltpu.make_async_copy(stem_h, stem, s_in.at[0])
    get_br = pltpu.make_async_copy(br_h, br, s_in.at[1])
    get_br.start()
    get_stem.start()
    barrier = pltpu.get_barrier_semaphore()
    line_x = [(c, mode_of((me["x"] + k) % 4, me["y"], me["z"])) for k in range(1, 4)]
    line_y = [(c, mode_of(me["x"], (me["y"] + k) % 4, me["z"])) for k in range(1, 4)]
    line_z = [(c, mode_of(me["x"], me["y"], (me["z"] + k) % 8)) for k in range(1, 8)]
    cuts = [((c + k) % 4, m) for k in range(1, 4)]

    def tell(sem, peers):
        for peer in peers:
            pl.semaphore_signal(sem, inc=1, device_id=peer, device_id_type=MESH)

    tell(barrier, line_x + line_y + line_z + cuts + [near("y", -1), near("y", 1), near("y", -2)])

    get_br.wait()
    for t in range(3):
        mine = br[order[t]]
        mine = jnp.where(core == 0, mine[:, :512], mine[:, 512:])
        MA[t, core, me["z"], me["x"], me["y"]] = mine[:, :128]
        for u in range(3):
            MB[t, core, u, me["x"], me["y"], me["z"]] = mine[:, 128 * (u + 1) : 128 * (u + 2)]

    lane = lax.broadcasted_iota(jnp.int32, (128, 1024), 1)

    def permute(t, put):
        for k in range(8):
            hot = (lane == idx[t, :, k : k + 1]).astype(F32).astype(BF)
            z = jnp.dot(hot, Y[...], preferred_element_type=F32)
            put(k, 0, z[:, :128].T)
            put(k, 1, z[:, 128:].T)

    def put_send(k, p, block):
        S[pl.ds(p * 8 + k, 128, stride=16), :] = block

    def exchange(send, recv, n, lo=1, hi=128):
        def go(i, carry):
            peer = far(i)
            pltpu.make_async_remote_copy(
                src_ref=send.at[peer], dst_ref=recv.at[m], send_sem=s_a2a.at[n], recv_sem=r_a2a.at[n],
                device_id=(c, peer), device_id_type=MESH,
            ).start()
            return carry

        lax.fori_loop(lo, hi, go, 0)

    def exchange_wait(send, recv, n):
        copy = pltpu.make_async_remote_copy(
            src_ref=send.at[pl.ds(0, 127)], dst_ref=recv.at[pl.ds(0, 127)], send_sem=s_a2a.at[n], recv_sem=r_a2a.at[n],
            device_id=(c, far(1)), device_id_type=MESH,
        )
        copy.wait_send()
        copy.wait_recv()

    partner = (yh * 2 + 1 - core, m)

    def share(t, kind, region):
        pltpu.make_async_remote_copy(
            src_ref=region, dst_ref=region, send_sem=s_p.at[t, min(kind, 1)], recv_sem=r_p.at[t, min(kind, 1)],
            device_id=partner, device_id_type=MESH,
        ).start()

    def gather_steps(t, kind):
        item = t * 3 + kind
        dims = ORDERS[kind]
        steps = []
        count = [0]
        waiting = []
        sent = []

        def region(ph, q, half=None):
            at = {}
            for d in "xyz":
                place = dims.index(d)
                if place < ph:
                    if half is not None and d == HALF[kind][ph]:
                        at[d] = pl.ds(half * (SIZE[d] // 2), SIZE[d] // 2)
                    else:
                        at[d] = pl.ds(0, SIZE[d])
                elif place == ph:
                    at[d] = q
                else:
                    at[d] = me[d]
            if kind == 0:
                return MA.at[t, core, at["z"], at["x"], at["y"]]
            return MB.at[t, core, pl.ds(*TILES[t][kind - 1]), at["x"], at["y"], at["z"]]

        def copy_of(ref, k, peer):
            return pltpu.make_async_remote_copy(
                src_ref=ref, dst_ref=ref, send_sem=s_ag.at[item, k], recv_sem=r_ag.at[item, k],
                device_id=peer, device_id_type=MESH,
            )

        def hop(d, step, src, landing):
            k = count[0]
            count[0] += 1
            copy = copy_of(src, k, near(d, step))
            copy.start()
            sent.append(copy)
            waiting.append((copy_of(landing, k, near(d, step)), landing))

        def direct(ph):
            d = dims[ph]
            k = count[0]
            count[0] += 1
            src = region(ph, me[d])
            for step in {"x": (1, 2, 3), "y": (1, -1, 2), "z": (1, 7, 2, 6, 3, 5, 4)}[d]:
                copy_of(src, k, near(d, step)).start()
            landing = region(ph, pl.ds(0, SIZE[d] - 1))
            arrive = copy_of(landing, k, near(d, 1))
            sent.append(arrive)
            waiting.append((arrive, None))

        def settle(last):
            for arrive, landing in waiting:
                arrive.wait_recv()
                if last:
                    share(t, kind, landing)
            waiting.clear()

        def make(ph, s):
            d = dims[ph]
            n = SIZE[d]
            q = me[d]
            top = n // 2 - 1

            def at(k):
                return (q + k + n) % n

            def step():
                settle(ph == 2 and s > 0)
                if ph == 2 and s == 0:
                    share(t, kind, region(2, q))
                if ph in DIRECT[kind]:
                    direct(ph)
                elif s < top:
                    hop(d, 1, region(ph, at(-s)), region(ph, at(-s - 1)))
                    hop(d, -1, region(ph, at(s)), region(ph, at(s + 1)))
                else:
                    hop(d, 1, region(ph, at(-s), 0), region(ph, at(-s - 1), 0))
                    hop(d, -1, region(ph, at(s), 1), region(ph, at(s + 1), 1))

            return step

        for ph in range(3):
            for s in range(1 if ph in DIRECT[kind] else SIZE[dims[ph]] // 2):
                steps.append(make(ph, s))
        steps.append(lambda: settle(True))

        def finish():
            for copy in sent:
                copy.wait_send()

        return steps, finish

    items = [[gather_steps(t, kind) for kind in range(3)] for t in range(3)]
    def gather_turn(turn):
        for t in range(3):
            for kind in range(3):
                steps = items[t][kind][0]
                s = turn - t * LAG
                if 0 <= s < len(steps):
                    steps[s]()

    n_turns = max(len(it[0]) for row in items for it in row) + 2 * LAG

    def share_wait(t):
        for n, buf in enumerate((MA, MB)):
            copy = pltpu.make_async_remote_copy(
                src_ref=buf.at[t, core], dst_ref=buf.at[t, 1 - core], send_sem=s_p.at[t, n], recv_sem=r_p.at[t, n],
                device_id=partner, device_id_type=MESH,
            )
            copy.wait_send()
            copy.wait_recv()

    pl.semaphore_wait(barrier, 19)
    gather_turn(0)
    tell(plane, line_y)
    get_stem.wait()
    Y[:, :128] = stem[0]
    Y[:, 128:] = stem[1]
    permute(0, put_send)
    snd1[...] = S[...].reshape(128, 16, 128).astype(BF)
    rcv1[m] = snd1[m]
    pl.semaphore_wait(plane, 3)
    tell(cube, line_x)
    gather_turn(1)
    pl.semaphore_wait(cube, 3)
    cut = [1, 33, 65, 97, 128]
    for turn in range(2, n_turns):
        if turn - 2 < 4:
            exchange(snd1, rcv1, 0, cut[turn - 2], cut[turn - 1])
        gather_turn(turn)

    def absorb(t):
        def part(g, carry):
            gx, gy = g // 2, g % 2
            o = None
            for h in range(2):
                tiles = [jnp.concatenate([MA[t, h, z, gx, gy * 2 + j] for j in range(2) for z in range(8)], axis=0)]
                tiles += [MB[t, h, u, gx, pl.ds(gy * 2, 2)].reshape(256, 128) for u in range(3)]
                part_o = jnp.dot(jnp.concatenate(tiles, axis=1), X[h * 512 : (h + 1) * 512], preferred_element_type=F32)
                o = part_o if o is None else o + part_o
            o = o.reshape(16, 16, 256)
            re = o[:, :8, :128] - o[:, 8:, 128:]
            im = o[:, :8, 128:] + o[:, 8:, :128]
            rows = pl.ds(pl.multiple_of(g * 128, 128), 128)
            Y[rows, :128] = re.reshape(128, 128).astype(BF)
            Y[rows, 128:] = im.reshape(128, 128).astype(BF)
            return carry

        lax.fori_loop(0, 8, part, 0)

    exchange_wait(snd1, rcv1, 0)
    first = rcv1[...].astype(F32)
    X[:, :128] = first[:, :8, :].reshape(1024, 128).astype(BF)
    X[:, 128:] = first[:, 8:, :].reshape(1024, 128).astype(BF)

    def put_next(k, p, block):
        S[pl.ds(p * 1024 + k, 128, stride=8), :] = block

    for t in range(3):
        if t > 0:
            permute(t, put_next)
            X[:, :128] = S[:1024].astype(BF)
            X[:, 128:] = S[1024:].astype(BF)
        share_wait(t)
        absorb(t)

    for p in range(2):
        for j in range(8):
            block = Y[j * 128 : (j + 1) * 128, p * 128 : (p + 1) * 128].astype(F32).T
            S[pl.ds(p * 8 + j, 128, stride=16), :] = block
            Y3T[p * 128 : (p + 1) * 128, j * 128 : (j + 1) * 128] = block.astype(BF)
    snd2[...] = S[...].reshape(128, 16, 128).astype(BF)
    exchange(snd2, rcv2, 1)
    rcv2[m] = snd2[m]

    state = lax.broadcasted_iota(jnp.int32, (1024, 512), 0)
    place = lax.broadcasted_iota(jnp.int32, (128, 512), 0)
    for q in range(4):
        rows = rb[:, q * 512 : (q + 1) * 512]
        cols = cb[:, q * 512 : (q + 1) * 512]
        hot = (state == rows).astype(F32).astype(BF)
        got = jnp.dot(Y3T[...], hot, preferred_element_type=F32)
        here = (place == cols // 128) & (cols % 128 == m)
        for p in range(2):
            val = jnp.sum(jnp.where(here, got[p * 128 : (p + 1) * 128], 0.0), axis=0, keepdims=True)
            a0[q, p : p + 1, :] = val

    def spread(src_of, buf, peers, mine, n):
        copies = []
        for k, peer in enumerate(peers):
            copy = pltpu.make_async_remote_copy(
                src_ref=src_of(k), dst_ref=buf.at[k + 1], send_sem=s_am.at[n, k], recv_sem=r_am.at[n, k],
                device_id=peer, device_id_type=MESH,
            )
            copy.start()
            copies.append(copy)
        buf[0] = mine
        for copy in copies:
            copy.wait()
        total = buf[0]
        for k in range(len(peers)):
            total = total + buf[k + 1]
        return total

    t1 = spread(lambda k: a0.at[(c + k + 1) % 4], a1, cuts, a0[c], 0)
    for g in range(4):
        a2[g, :, :] = t1[:, g * 128 : (g + 1) * 128]
    mx = me["x"]
    t2 = spread(
        lambda k: a2.at[(mx + k + 1) % 4], a3,
        line_x, a2[mx], 1,
    )
    a2[4] = t2
    t3 = spread(
        lambda k: a2.at[4], a3.at[pl.ds(4, 4)],
        line_y, t2, 2,
    )
    a2[5] = t3
    t4 = spread(
        lambda k: a2.at[5], a4,
        line_z, t3, 3,
    )
    amp[...] = t4

    for t in range(3):
        for kind in range(3):
            items[t][kind][1]()
    exchange_wait(snd2, rcv2, 1)
    S[...] = rcv2[...].astype(F32).reshape(2048, 128)
    for p in range(2):
        for j in range(8):
            block = S[pl.ds(p * 8 + j, 128, stride=16), :]
            out[p, j * 128 : (j + 1) * 128, :] = block.T.astype(BF)


def body(stem, branches, order, swap_order, row_bits, column_bits):
    vmem = pl.BlockSpec(memory_space=pltpu.VMEM)
    br = branches.transpose(0, 1, 3, 2).reshape(3, 16, 1024)
    idx = swap_order.reshape(3, 128, 8)
    dma = pltpu.SemaphoreType.DMA
    field, amps = pl.pallas_call(
        kernel,
        out_shape=(jax.ShapeDtypeStruct((2, 1024, 128), BF), jax.ShapeDtypeStruct((2, 128), F32)),
        in_specs=[pl.BlockSpec(memory_space=pltpu.SMEM)] + [pl.BlockSpec(memory_space=pltpu.HBM)] * 2 + [vmem] * 3,
        out_specs=(vmem, vmem),
        scratch_shapes=[
            pltpu.VMEM((2, 1024, 128), BF),
            pltpu.VMEM((3, 16, 1024), BF),
            pltpu.VMEM((3, 2, 8, 4, 4, 16, 128), BF),
            pltpu.VMEM((3, 2, 3, 4, 4, 8, 16, 128), BF),
            pltpu.VMEM((1024, 256), BF),
            pltpu.VMEM((1024, 256), BF),
            pltpu.VMEM((2048, 128), F32),
            pltpu.VMEM((256, 1024), BF),
            pltpu.VMEM((128, 16, 128), BF),
            pltpu.VMEM((128, 16, 128), BF),
            pltpu.VMEM((128, 16, 128), BF),
            pltpu.VMEM((128, 16, 128), BF),
            pltpu.VMEM((4, 2, 512), F32),
            pltpu.VMEM((4, 2, 512), F32),
            pltpu.VMEM((6, 2, 128), F32),
            pltpu.VMEM((8, 2, 128), F32),
            pltpu.VMEM((8, 2, 128), F32),
            dma((2,)), dma((2,)),
            dma((9, 12)), dma((9, 12)),
            dma((3, 2)), dma((3, 2)),
            dma((4, 7)), dma((4, 7)),
            dma((2,)),
            pltpu.SemaphoreType.REGULAR, pltpu.SemaphoreType.REGULAR,
        ],
        compiler_params=pltpu.CompilerParams(collective_id=0, has_side_effects=True, vmem_limit_bytes=48 * 1024 * 1024),
    )(order, stem[0], br, idx, row_bits.reshape(1, 2048), column_bits.reshape(1, 2048))
    m = lax.axis_index("mode")
    amps = lax.dynamic_slice_in_dim(amps, (m % 32) * 4, 4, 1)
    return field[None], amps


def solution(mesh):
    placed = (P("cuts", None, None, "mode"), P(None, None, None, "mode"), P(), P(), P(), P())
    return jax.shard_map(
        body,
        mesh=mesh,
        in_specs=placed,
        out_specs=(P("cuts", None, None, "mode"), P(None, ("cuts", "mode"))),
        check_vma=False,
    )
```

```python
import functools

import jax
import jax.numpy as jnp
from jax import lax
from jax.experimental import pallas as pl
from jax.experimental.pallas import tpu as pltpu
from jax.sharding import PartitionSpec as P

MESH = pl.DeviceIdType.MESH
BF = jnp.bfloat16
F32 = jnp.float32
SIZE = {"x": 4, "y": 4, "z": 8}
ORDERS = ("xyz", "zyx", "zxy")
DIRECT = ((0, 1), (0,), (0,))
HALF = (("", "", "x"), ("", "z", "y"), ("", "z", "x"))
TILES = (((0, 0), (0, 2), (2, 2)), ((0, 2), (4, 1), (5, 1)), ((2, 1), (6, 2), (8, 1)))
RATE = 46.0
FLY = 2.0


def plan(tasks):
    now, free, done, ready_at, order = 0.0, {}, set(), {}, []
    left = list(tasks)
    while left:
        best = None
        for task in left:
            if any(dep not in ready_at for dep in task["deps"]):
                continue
            when = max([task["start"]] + [ready_at[dep] for dep in task["deps"]])
            score = (max(when, now), task["rank"])
            if best is None or score < best[0]:
                best = (score, task)
        (when, _), task = best
        left.remove(task)
        now = when + task["cost"]
        end = now
        for link, size in task["loads"].items():
            free[link] = max(free.get(link, 0.0), now) + size / RATE
            end = max(end, free[link])
        ready_at[task["key"]] = end + (FLY if task["loads"] else 0.0)
        order.append(task)
    return order


def kernel(order, stem_h, br_h, idx, rb, cb, out, amp, stem, br, MA, MB, PT, RT, Y, X, S, Y3T, snd1, rcv1, snd2, rcv2, a0, a1, a2, a3,
           s_a2a, r_a2a, s_ag, r_ag, s_p, r_p, s_am, r_am, s_in, plane, cube, square):
    c = lax.axis_index("cuts")
    m = lax.axis_index("mode")
    core, yh = c % 2, c // 2
    me = {"x": m // 32, "y": (m // 8) % 4, "z": m % 8}
    yg = yh * 4 + me["y"]

    def mode_of(x, y, z):
        return x * 32 + y * 8 + z

    def near(d, step):
        if d == "x":
            return c, mode_of((me["x"] + step + 4) % 4, me["y"], me["z"])
        if d == "z":
            return c, mode_of(me["x"], me["y"], (me["z"] + step + 8) % 8)
        g = (yg + step + 8) % 8
        return (g // 4) * 2 + core, mode_of(me["x"], g % 4, me["z"])

    def far(i):
        k = (i * 37) % 128
        return mode_of((me["x"] + k // 32) % 4, (me["y"] + (k // 8) % 4) % 4, (me["z"] + k % 8) % 8)

    get_stem = pltpu.make_async_copy(stem_h, stem, s_in.at[0])
    get_br = pltpu.make_async_copy(br_h, br, s_in.at[1])
    get_br.start()
    get_stem.start()
    barrier = pltpu.get_barrier_semaphore()
    line_x = [(c, mode_of((me["x"] + k) % 4, me["y"], me["z"])) for k in range(1, 4)]
    line_y = [(c, mode_of(me["x"], (me["y"] + k) % 4, me["z"])) for k in range(1, 4)]
    line_z = [(c, mode_of(me["x"], me["y"], (me["z"] + k) % 8)) for k in range(1, 8)]
    cuts = [((c + k) % 4, m) for k in range(1, 4)]

    def tell(sem, peers):
        for peer in peers:
            pl.semaphore_signal(sem, inc=1, device_id=peer, device_id_type=MESH)

    tell(barrier, line_x + line_y + line_z + cuts + [near("y", -1), near("y", 1), near("y", -2)])

    get_br.wait()
    for t in range(3):
        mine = br[order[t]]
        mine = jnp.where(core == 0, mine[:, :512], mine[:, 512:])
        u = 0
        for kind in range(3):
            for tile in range(TILES[t][kind][0], sum(TILES[t][kind])):
                part = mine[:, 128 * u : 128 * (u + 1)]
                u += 1
                if kind == 0:
                    MA[core, tile, me["z"], me["x"], me["y"]] = part
                else:
                    MB[core, tile, me["x"], me["y"], me["z"]] = part

    lane = lax.broadcasted_iota(jnp.int32, (128, 1024), 1)

    def table(t, k):
        return (lane == idx[t, :, k : k + 1]).astype(F32).astype(BF)

    def permute(t, put, ks):
        for k in ks:
            hot = table(t, k) if t == 0 else PT[t - 1, k * 128 : (k + 1) * 128, :]
            z = jnp.dot(hot, Y[...], preferred_element_type=F32)
            put(k, 0, z[:, :128].T)
            put(k, 1, z[:, 128:].T)

    state = lax.broadcasted_iota(jnp.int32, (1024, 256), 0)

    def make_pt(t, ks):
        for k in ks:
            PT[t - 1, k * 128 : (k + 1) * 128, :] = table(t, k)

    def make_rt(qs):
        for q in qs:
            RT[q] = (state == rb[:, q * 256 : (q + 1) * 256]).astype(F32).astype(BF)

    def put_send(k, p, block):
        S[pl.ds(p * 8 + k, 128, stride=16), :] = block

    def exchange(send, recv, n, lo=1, hi=128):
        def go(i, carry):
            peer = far(i)
            pltpu.make_async_remote_copy(
                src_ref=send.at[peer], dst_ref=recv.at[m], send_sem=s_a2a.at[n], recv_sem=r_a2a.at[n],
                device_id=(c, peer), device_id_type=MESH,
            ).start()
            return carry

        lax.fori_loop(lo, hi, go, 0)

    def exchange_wait(send, recv, n):
        copy = pltpu.make_async_remote_copy(
            src_ref=send.at[pl.ds(0, 127)], dst_ref=recv.at[pl.ds(0, 127)], send_sem=s_a2a.at[n], recv_sem=r_a2a.at[n],
            device_id=(c, far(1)), device_id_type=MESH,
        )
        copy.wait_send()
        copy.wait_recv()

    partner = (yh * 2 + 1 - core, m)

    def share(t, kind, region):
        pltpu.make_async_remote_copy(
            src_ref=region, dst_ref=region, send_sem=s_p.at[t, min(kind, 1)], recv_sem=r_p.at[t, min(kind, 1)],
            device_id=partner, device_id_type=MESH,
        ).start()

    tasks = []
    fns = {}
    seen = set()
    sent = []
    arrivals = {}

    def add(key, deps, fn, cost=0.08, loads=None, rank=0, start=0.0):
        tasks.append(dict(key=key, deps=deps, cost=cost, loads=loads or {}, rank=rank, start=start))
        fns[key] = fn

    def land(keys):
        for key in keys:
            if key in arrivals and key not in seen:
                seen.add(key)
                arrivals[key].wait_recv()

    def gather_item(t, kind):
        item = t * 3 + kind
        dims = ORDERS[kind]
        count = [0]
        width = TILES[t][kind][1]

        def region(ph, q, half=None):
            at = {}
            for d in "xyz":
                place = dims.index(d)
                if place < ph:
                    if half is not None and d == HALF[kind][ph]:
                        at[d] = pl.ds(half * (SIZE[d] // 2), SIZE[d] // 2)
                    else:
                        at[d] = pl.ds(0, SIZE[d])
                elif place == ph:
                    at[d] = q
                else:
                    at[d] = me[d]
            if kind == 0:
                return MA.at[core, pl.ds(*TILES[t][kind]), at["z"], at["x"], at["y"]]
            return MB.at[core, pl.ds(*TILES[t][kind]), at["x"], at["y"], at["z"]]

        def copy_of(ref, k, peer):
            return pltpu.make_async_remote_copy(
                src_ref=ref, dst_ref=ref, send_sem=s_ag.at[item, k], recv_sem=r_ag.at[item, k],
                device_id=peer, device_id_type=MESH,
            )

        def hop(ph, step, piece, half, deps, key):
            d = dims[ph]
            n = SIZE[d]
            k = count[0]
            count[0] += 1
            src = region(ph, (me[d] + piece + n) % n, half)
            landing = region(ph, (me[d] + piece - step + n) % n, half)
            arrivals[key] = copy_of(landing, k, near(d, step))
            size = 4 * width * (1 if half is None else 0.5)
            for done in dims[:ph]:
                size *= SIZE[done]

            def fn():
                land(deps)
                copy = copy_of(src, k, near(d, step))
                copy.start()
                sent.append(copy)

            add(key, deps, fn, loads={(d, step): size}, rank=t * 10 + ph)
            if ph == 2:

                def hand():
                    land([key])
                    share(t, kind, landing)

                add(key + ("share",), [key], hand, rank=t * 10 + 5, loads={("core", 1): size / 8})
            return key

        def direct(ph, deps, key):
            d = dims[ph]
            k = count[0]
            count[0] += 1
            src = region(ph, me[d])
            landing = region(ph, pl.ds(0, SIZE[d] - 1))
            arrivals[key] = copy_of(landing, k, near(d, 1))
            size = 4.0 * width * (1 if ph == 0 else 4) * {"x": 2, "y": 2, "z": 8}[d]

            def fn():
                land(deps)
                for step in {"x": (1, 2, 3), "y": (1, -1, 2), "z": (1, 7, 2, 6, 3, 5, 4)}[d]:
                    copy_of(src, k, near(d, step)).start()
                sent.append(arrivals[key])

            add(key, deps, fn, cost=0.3, loads={(d, 1): size, (d, -1): size}, rank=t * 10 + ph)
            return key

        def ring(ph, deps):
            d = dims[ph]
            tag = (t, kind, ph)
            out = []
            if SIZE[d] == 8:
                r, l = deps, deps
                for s in range(3):
                    r = [hop(ph, 1, -s, None, r, tag + ("r", s))]
                    l = [hop(ph, -1, s, None, l, tag + ("l", s))]
                    out += r + l
                out.append(hop(ph, 1, -3, 0, r, tag + ("r", 3)))
                out.append(hop(ph, -1, 3, 1, l, tag + ("l", 3)))
            elif ph == 2:
                r = hop(ph, 1, 0, 0, deps, tag + ("r", 0))
                l = hop(ph, -1, 0, 1, deps, tag + ("l", 0))
                out += [r, l, hop(ph, 1, 0, 1, deps, tag + ("r", 1)), hop(ph, -1, 0, 0, deps, tag + ("l", 1))]
                out += [hop(ph, 1, -1, 0, [r], tag + ("r", 2)), hop(ph, -1, 1, 1, [l], tag + ("l", 2))]
            else:
                r = hop(ph, 1, 0, None, deps, tag + ("r", 0))
                l = hop(ph, -1, 0, None, deps, tag + ("l", 0))
                out += [r, l, hop(ph, 1, -1, 0, [r], tag + ("r", 1)), hop(ph, -1, 1, 1, [l], tag + ("l", 1))]
            return out

        first = [direct(0, [], (t, kind, 0, "d"))]
        second = [direct(1, first, (t, kind, 1, "d"))] if 1 in DIRECT[kind] else ring(1, first)

        def hand_own():
            land(second)
            share(t, kind, region(2, me[dims[2]]))

        add((t, kind, 2, "own"), second, hand_own, rank=t * 10 + 4, loads={("core", 1): 16.0 * width})
        third = ring(2, second)
        return [(t, kind, 2, "own")] + [key + ("share",) for key in third]

    def share_wait(t):
        spans = ((MA, TILES[t][0]), (MB, (TILES[t][1][0], TILES[t][1][1] + TILES[t][2][1])))
        for n, (buf, span) in enumerate(spans):
            if span[1] == 0:
                continue
            copy = pltpu.make_async_remote_copy(
                src_ref=buf.at[core, pl.ds(*span)], dst_ref=buf.at[1 - core, pl.ds(*span)],
                send_sem=s_p.at[t, n], recv_sem=r_p.at[t, n], device_id=partner, device_id_type=MESH,
            )
            copy.wait_send()
            copy.wait_recv()

    def absorb(t, gs):
        for g in gs:
            gx, gy = g // 2, g % 2
            o = None
            for h in range(2):
                tiles = []
                for kind in range(3):
                    for u in range(TILES[t][kind][0], sum(TILES[t][kind])):
                        if kind == 0:
                            rows = [MA[h, u, z, gx, gy * 2 + j] for j in range(2) for z in range(8)]
                            tiles.append(jnp.concatenate(rows, axis=0))
                        else:
                            tiles.append(MB[h, u, gx, gy * 2 : gy * 2 + 2].reshape(256, 128))
                part_o = jnp.dot(jnp.concatenate(tiles, axis=1), X[h * 512 : (h + 1) * 512], preferred_element_type=F32)
                o = part_o if o is None else o + part_o
            o = o.reshape(16, 16, 256)
            re = o[:, :8, :128] - o[:, 8:, 128:]
            im = o[:, :8, 128:] + o[:, 8:, :128]
            Y[g * 128 : (g + 1) * 128, :128] = re.reshape(128, 128).astype(BF)
            Y[g * 128 : (g + 1) * 128, 128:] = im.reshape(128, 128).astype(BF)

    def put_next(k, p, block):
        S[pl.ds(p * 1024 + k, 128, stride=8), :] = block

    def enter():
        pl.semaphore_wait(barrier, 19)

    def to_plane():
        tell(plane, line_y)
        tell(square, cuts)

    def prepare_in():
        get_stem.wait()
        Y[:, :128] = stem[0]
        Y[:, 128:] = stem[1]

    def to_cube():
        pl.semaphore_wait(plane, 3)
        tell(cube, line_x)

    def all_in():
        pl.semaphore_wait(cube, 3)

    def prepare_out():
        snd1[...] = S[...].reshape(128, 16, 128).astype(BF)
        rcv1[m] = snd1[m]

    def start(t):
        if t == 0:
            exchange_wait(snd1, rcv1, 0)
            got = rcv1[...].astype(F32)
            X[:, :128] = got[:, :8, :].reshape(1024, 128).astype(BF)
            X[:, 128:] = got[:, 8:, :].reshape(1024, 128).astype(BF)
        else:
            X[:, :128] = S[:1024].astype(BF)
            X[:, 128:] = S[1024:].astype(BF)
        share_wait(t)

    pairs = ((0, 1), (2, 3), (4, 5), (6, 7))
    enter()
    shares = {}
    for t in range(3):
        shares[t] = []
        for kind in range(3):
            if TILES[t][kind][1] > 0:
                shares[t] += gather_item(t, kind)
    add("plane", [], to_plane, rank=1, start=0.5)
    add("in", [], prepare_in, rank=2, cost=0.3, start=0.6)
    last = ["in"]
    for n, ks in enumerate(pairs):
        add(("p", 0, n), last, functools.partial(permute, 0, put_send, ks), rank=2, cost=0.7)
        last = [("p", 0, n)]
    add("out", last, prepare_out, rank=2, cost=0.4)
    add("cube", ["plane"], to_cube, rank=2, start=3.5)
    add("all", ["cube"], all_in, rank=3, start=6.0)
    last = ["all", "out"]
    for n in range(8):
        lo, hi = max(1, n * 16), (n + 1) * 16
        add(("x", n), last, functools.partial(exchange, snd1, rcv1, 0, lo, hi), cost=0.6, rank=3,
            loads={(d, w): {"x": 40, "y": 64, "z": 80}[d] for d in "xyz" for w in (1, -1)}, start=6.0 + 0.8 * n)
    for n in range(4):
        add(("t", 1, n), [], functools.partial(make_pt, 1, pairs[n]), rank=50, cost=0.3, start=7.0)
        add(("t", 2, n), [], functools.partial(make_pt, 2, pairs[n]), rank=51, cost=0.3, start=7.0)
        add(("t", 3, n), [], functools.partial(make_rt, pairs[n]), rank=52, cost=0.4, start=7.0)
    ready = [("x", n) for n in range(8)]
    for t in range(3):
        add(("s", t), shares[t] + ready, functools.partial(start, t), cost=1.0, rank=30, start=0.0)
        last = [("s", t)]
        for n, gs in enumerate(pairs):
            add(("m", t, n), last, functools.partial(absorb, t, gs), cost=0.5, rank=30)
            last = [("m", t, n)]
        if t < 2:
            for n, ks in enumerate(pairs):
                add(("p", t + 1, n), last + [("t", t + 1, n)], functools.partial(permute, t + 1, put_next, ks), cost=0.5, rank=30)
                last = [("p", t + 1, n)]
        ready = last
    ordered = plan(tasks)
    for task in ordered:
        fns[task["key"]]()

    for p in range(2):
        for j in range(8):
            block = Y[j * 128 : (j + 1) * 128, p * 128 : (p + 1) * 128].astype(F32).T
            S[pl.ds(p * 8 + j, 128, stride=16), :] = block
            Y3T[p * 128 : (p + 1) * 128, j * 128 : (j + 1) * 128] = block.astype(BF)
    snd2[...] = S[...].reshape(128, 16, 128).astype(BF)
    exchange(snd2, rcv2, 1, 1, 64)
    rcv2[m] = snd2[m]

    place = lax.broadcasted_iota(jnp.int32, (128, 256), 0)
    for q in range(8):
        cols = cb[:, q * 256 : (q + 1) * 256]
        got = jnp.dot(Y3T[...], RT[q], preferred_element_type=F32)
        here = (place == cols // 128) & (cols % 128 == m)
        for p in range(2):
            val = jnp.sum(jnp.where(here, got[p * 128 : (p + 1) * 128], 0.0), axis=0, keepdims=True)
            a0[q * 2, p : p + 1, :] = val[:, :128]
            a0[q * 2 + 1, p : p + 1, :] = val[:, 128:]

    def spread(src_of, buf, peers, n):
        copies = []
        for k, peer in enumerate(peers):
            copy = pltpu.make_async_remote_copy(
                src_ref=src_of(k), dst_ref=buf.at[k + 1], send_sem=s_am.at[n, k], recv_sem=r_am.at[n, k],
                device_id=peer, device_id_type=MESH,
            )
            copy.start()
            copies.append(copy)
        return copies

    def collect(buf, copies, mine):
        total = mine
        for copy in copies:
            copy.wait()
        for k in range(len(copies)):
            total = total + buf[k + 1]
        return total

    pl.semaphore_wait(square, 3)
    face = [((c + i) % 4, (me["x"] + j) % 4) for i in range(4) for j in range(4) if i + j > 0]
    sheet = [((me["y"] + i) % 4, (me["z"] + j) % 8) for i in range(4) for j in range(8) if i + j > 0]
    one = spread(lambda k: a0.at[face[k][0] * 4 + face[k][1]], a1, [(i, mode_of(j, me["y"], me["z"])) for i, j in face], 0)
    exchange(snd2, rcv2, 1, 64, 128)
    a2[...] = collect(a1, one, a0[c * 4 + me["x"]])
    two = spread(lambda k: a2, a3, [(c, mode_of(me["x"], i, j)) for i, j in sheet], 1)
    for copy in sent:
        copy.wait_send()
    amp[...] = collect(a3, two, a2[...])

    exchange_wait(snd2, rcv2, 1)
    S[...] = rcv2[...].astype(F32).reshape(2048, 128)
    for p in range(2):
        for j in range(8):
            block = S[pl.ds(p * 8 + j, 128, stride=16), :]
            out[p, j * 128 : (j + 1) * 128, :] = block.T.astype(BF)


def body(stem, branches, order, swap_order, row_bits, column_bits):
    vmem = pl.BlockSpec(memory_space=pltpu.VMEM)
    br = branches.transpose(0, 1, 3, 2).reshape(3, 16, 1024)
    idx = swap_order.reshape(3, 128, 8)
    dma = pltpu.SemaphoreType.DMA
    field, amps = pl.pallas_call(
        kernel,
        out_shape=(jax.ShapeDtypeStruct((2, 1024, 128), BF), jax.ShapeDtypeStruct((2, 128), F32)),
        in_specs=[pl.BlockSpec(memory_space=pltpu.SMEM)] + [pl.BlockSpec(memory_space=pltpu.HBM)] * 2 + [vmem] * 3,
        out_specs=(vmem, vmem),
        scratch_shapes=[
            pltpu.VMEM((2, 1024, 128), BF),
            pltpu.VMEM((3, 16, 1024), BF),
            pltpu.VMEM((2, 3, 8, 4, 4, 16, 128), BF),
            pltpu.VMEM((2, 9, 4, 4, 8, 16, 128), BF),
            pltpu.VMEM((2, 1024, 1024), BF),
            pltpu.VMEM((8, 1024, 256), BF),
            pltpu.VMEM((1024, 256), BF),
            pltpu.VMEM((1024, 256), BF),
            pltpu.VMEM((2048, 128), F32),
            pltpu.VMEM((256, 1024), BF),
            pltpu.VMEM((128, 16, 128), BF),
            pltpu.VMEM((128, 16, 128), BF),
            pltpu.VMEM((128, 16, 128), BF),
            pltpu.VMEM((128, 16, 128), BF),
            pltpu.VMEM((16, 2, 128), F32),
            pltpu.VMEM((16, 2, 128), F32),
            pltpu.VMEM((2, 128), F32),
            pltpu.VMEM((32, 2, 128), F32),
            dma((2,)), dma((2,)),
            dma((9, 12)), dma((9, 12)),
            dma((3, 2)), dma((3, 2)),
            dma((2, 31)), dma((2, 31)),
            dma((2,)),
            pltpu.SemaphoreType.REGULAR, pltpu.SemaphoreType.REGULAR, pltpu.SemaphoreType.REGULAR,
        ],
        compiler_params=pltpu.CompilerParams(collective_id=0, has_side_effects=True, vmem_limit_bytes=63_000_000),
    )(order, stem[0], br, idx, row_bits.reshape(1, 2048), column_bits.reshape(1, 2048))
    m = lax.axis_index("mode")
    amps = lax.dynamic_slice_in_dim(amps, (m % 32) * 4, 4, 1)
    return field[None], amps


def solution(mesh):
    placed = (P("cuts", None, None, "mode"), P(None, None, None, "mode"), P(), P(), P(), P())
    return jax.shard_map(
        body,
        mesh=mesh,
        in_specs=placed,
        out_specs=(P("cuts", None, None, "mode"), P(None, ("cuts", "mode"))),
        check_vma=False,
    )
```

```python
import functools

import jax
import jax.numpy as jnp
from jax import lax
from jax.experimental import pallas as pl
from jax.experimental.pallas import tpu as pltpu
from jax.sharding import PartitionSpec as P

MESH = pl.DeviceIdType.MESH
BF = jnp.bfloat16
F32 = jnp.float32
SIZE = {"x": 4, "y": 4, "z": 8}
ORDERS = ("xyz", "zyx", "zxy")
DIRECT = ((0, 1), (0,), (0,))
HALF = (("", "", "x"), ("", "z", "y"), ("", "z", "x"))
TILES = (((0, 0), (0, 2), (2, 2)), ((0, 2), (4, 1), (5, 1)), ((2, 1), (6, 2), (8, 1)))
RATE = 46.0
FLY = 2.0


def plan(tasks):
    now, free, done, ready_at, order = 0.0, {}, set(), {}, []
    left = list(tasks)
    while left:
        best = None
        for task in left:
            if any(dep not in ready_at for dep in task["deps"]):
                continue
            when = max([task["start"]] + [ready_at[dep] for dep in task["deps"]])
            score = (max(when, now), task["rank"])
            if best is None or score < best[0]:
                best = (score, task)
        (when, _), task = best
        left.remove(task)
        now = when + task["cost"]
        end = now
        for link, size in task["loads"].items():
            free[link] = max(free.get(link, 0.0), now) + size / RATE
            end = max(end, free[link])
        ready_at[task["key"]] = end + (FLY if task["loads"] else 0.0)
        order.append(task)
    return order


def kernel(order, stem_h, br_h, idx, rb, cb, out, amp, stem, br, MA, MB, PT, RT, Y, X, S, Y3T, snd1, rcv1, snd2, rcv2, a0, a1, a2, a3,
           s_a2a, r_a2a, s_ag, r_ag, s_p, r_p, s_am, r_am, s_in, plane, cube, square):
    c = lax.axis_index("cuts")
    m = lax.axis_index("mode")
    core, yh = c % 2, c // 2
    me = {"x": m // 32, "y": (m // 8) % 4, "z": m % 8}
    yg = yh * 4 + me["y"]

    def mode_of(x, y, z):
        return x * 32 + y * 8 + z

    def near(d, step):
        if d == "x":
            return c, mode_of((me["x"] + step + 4) % 4, me["y"], me["z"])
        if d == "z":
            return c, mode_of(me["x"], me["y"], (me["z"] + step + 8) % 8)
        g = (yg + step + 8) % 8
        return (g // 4) * 2 + core, mode_of(me["x"], g % 4, me["z"])

    def far(i):
        k = (i * 37) % 128
        return mode_of((me["x"] + k // 32) % 4, (me["y"] + (k // 8) % 4) % 4, (me["z"] + k % 8) % 8)

    get_stem = pltpu.make_async_copy(stem_h, stem, s_in.at[0])
    get_br = pltpu.make_async_copy(br_h, br, s_in.at[1])
    get_br.start()
    get_stem.start()
    barrier = pltpu.get_barrier_semaphore()
    line_x = [(c, mode_of((me["x"] + k) % 4, me["y"], me["z"])) for k in range(1, 4)]
    line_y = [(c, mode_of(me["x"], (me["y"] + k) % 4, me["z"])) for k in range(1, 4)]
    line_z = [(c, mode_of(me["x"], me["y"], (me["z"] + k) % 8)) for k in range(1, 8)]
    cuts = [((c + k) % 4, m) for k in range(1, 4)]

    def tell(sem, peers):
        for peer in peers:
            pl.semaphore_signal(sem, inc=1, device_id=peer, device_id_type=MESH)

    tell(barrier, line_x + line_y + line_z + cuts + [near("y", -1), near("y", 1), near("y", -2)])

    get_br.wait()
    for t in range(3):
        mine = br[order[t]]
        mine = jnp.where(core == 0, mine[:, :512], mine[:, 512:])
        u = 0
        for kind in range(3):
            for tile in range(TILES[t][kind][0], sum(TILES[t][kind])):
                part = mine[:, 128 * u : 128 * (u + 1)]
                u += 1
                if kind == 0:
                    MA[core, tile, me["z"], me["x"], me["y"]] = part
                else:
                    MB[core, tile, me["x"], me["y"], me["z"]] = part

    lane = lax.broadcasted_iota(jnp.int32, (128, 1024), 1)

    def table(t, k):
        return (lane == idx[t, :, k : k + 1]).astype(F32).astype(BF)

    def permute(t, put, ks):
        for k in ks:
            hot = table(t, k) if t == 0 else PT[t - 1, k * 128 : (k + 1) * 128, :]
            z = jnp.dot(hot, Y[...], preferred_element_type=F32)
            put(k, 0, z[:, :128].T)
            put(k, 1, z[:, 128:].T)

    state = lax.broadcasted_iota(jnp.int32, (1024, 256), 0)

    def make_pt(t, ks):
        for k in ks:
            PT[t - 1, k * 128 : (k + 1) * 128, :] = table(t, k)

    def make_rt(qs):
        for q in qs:
            RT[q] = (state == rb[:, q * 256 : (q + 1) * 256]).astype(F32).astype(BF)

    def put_send(k, p, block):
        S[pl.ds(p * 8 + k, 128, stride=16), :] = block

    def exchange(send, recv, n, lo=1, hi=128):
        def go(i, carry):
            peer = far(i)
            pltpu.make_async_remote_copy(
                src_ref=send.at[peer], dst_ref=recv.at[m], send_sem=s_a2a.at[n], recv_sem=r_a2a.at[n],
                device_id=(c, peer), device_id_type=MESH,
            ).start()
            return carry

        lax.fori_loop(lo, hi, go, 0)

    def exchange_wait(send, recv, n):
        copy = pltpu.make_async_remote_copy(
            src_ref=send.at[pl.ds(0, 127)], dst_ref=recv.at[pl.ds(0, 127)], send_sem=s_a2a.at[n], recv_sem=r_a2a.at[n],
            device_id=(c, far(1)), device_id_type=MESH,
        )
        copy.wait_send()
        copy.wait_recv()

    partner = (yh * 2 + 1 - core, m)

    def share(t, kind, region):
        pltpu.make_async_remote_copy(
            src_ref=region, dst_ref=region, send_sem=s_p.at[t, min(kind, 1)], recv_sem=r_p.at[t, min(kind, 1)],
            device_id=partner, device_id_type=MESH,
        ).start()

    tasks = []
    fns = {}
    seen = set()
    sent = []
    arrivals = {}

    def add(key, deps, fn, cost=0.08, loads=None, rank=0, start=0.0):
        tasks.append(dict(key=key, deps=deps, cost=cost, loads=loads or {}, rank=rank, start=start))
        fns[key] = fn

    def land(keys):
        for key in keys:
            if key in arrivals and key not in seen:
                seen.add(key)
                arrivals[key].wait_recv()

    def gather_item(t, kind):
        item = t * 3 + kind
        dims = ORDERS[kind]
        count = [0]
        width = TILES[t][kind][1]

        def region(ph, q, half=None):
            at = {}
            for d in "xyz":
                place = dims.index(d)
                if place < ph:
                    if half is not None and d == HALF[kind][ph]:
                        at[d] = pl.ds(half * (SIZE[d] // 2), SIZE[d] // 2)
                    else:
                        at[d] = pl.ds(0, SIZE[d])
                elif place == ph:
                    at[d] = q
                else:
                    at[d] = me[d]
            if kind == 0:
                return MA.at[core, pl.ds(*TILES[t][kind]), at["z"], at["x"], at["y"]]
            return MB.at[core, pl.ds(*TILES[t][kind]), at["x"], at["y"], at["z"]]

        def copy_of(ref, k, peer):
            return pltpu.make_async_remote_copy(
                src_ref=ref, dst_ref=ref, send_sem=s_ag.at[item, k], recv_sem=r_ag.at[item, k],
                device_id=peer, device_id_type=MESH,
            )

        def hop(ph, step, piece, half, deps, key):
            d = dims[ph]
            n = SIZE[d]
            k = count[0]
            count[0] += 1
            src = region(ph, (me[d] + piece + n) % n, half)
            landing = region(ph, (me[d] + piece - step + n) % n, half)
            arrivals[key] = copy_of(landing, k, near(d, step))
            size = 4 * width * (1 if half is None else 0.5)
            for done in dims[:ph]:
                size *= SIZE[done]

            def fn():
                land(deps)
                copy = copy_of(src, k, near(d, step))
                copy.start()
                sent.append(copy)

            add(key, deps, fn, loads={(d, step): size}, rank=t * 10 + ph)
            if ph == 2:

                def hand():
                    land([key])
                    share(t, kind, landing)

                add(key + ("share",), [key], hand, rank=t * 10 + 5, loads={("core", 1): size / 8})
            return key

        def direct(ph, deps, key):
            d = dims[ph]
            k = count[0]
            count[0] += 1
            src = region(ph, me[d])
            landing = region(ph, pl.ds(0, SIZE[d] - 1))
            arrivals[key] = copy_of(landing, k, near(d, 1))
            size = 4.0 * width * (1 if ph == 0 else 4) * {"x": 2, "y": 2, "z": 8}[d]

            def fn():
                land(deps)
                for step in {"x": (1, 2, 3), "y": (1, -1, 2), "z": (1, 7, 2, 6, 3, 5, 4)}[d]:
                    copy_of(src, k, near(d, step)).start()
                sent.append(arrivals[key])

            add(key, deps, fn, cost=0.3, loads={(d, 1): size, (d, -1): size}, rank=t * 10 + ph)
            return key

        def ring(ph, deps):
            d = dims[ph]
            tag = (t, kind, ph)
            out = []
            if SIZE[d] == 8:
                r, l = deps, deps
                for s in range(3):
                    r = [hop(ph, 1, -s, None, r, tag + ("r", s))]
                    l = [hop(ph, -1, s, None, l, tag + ("l", s))]
                    out += r + l
                out.append(hop(ph, 1, -3, 0, r, tag + ("r", 3)))
                out.append(hop(ph, -1, 3, 1, l, tag + ("l", 3)))
            elif ph == 2:
                r = hop(ph, 1, 0, 0, deps, tag + ("r", 0))
                l = hop(ph, -1, 0, 1, deps, tag + ("l", 0))
                out += [r, l, hop(ph, 1, 0, 1, deps, tag + ("r", 1)), hop(ph, -1, 0, 0, deps, tag + ("l", 1))]
                out += [hop(ph, 1, -1, 0, [r], tag + ("r", 2)), hop(ph, -1, 1, 1, [l], tag + ("l", 2))]
            else:
                r = hop(ph, 1, 0, None, deps, tag + ("r", 0))
                l = hop(ph, -1, 0, None, deps, tag + ("l", 0))
                out += [r, l, hop(ph, 1, -1, 0, [r], tag + ("r", 1)), hop(ph, -1, 1, 1, [l], tag + ("l", 1))]
            return out

        first = [direct(0, [], (t, kind, 0, "d"))]
        second = [direct(1, first, (t, kind, 1, "d"))] if 1 in DIRECT[kind] else ring(1, first)

        def hand_own():
            land(second)
            share(t, kind, region(2, me[dims[2]]))

        add((t, kind, 2, "own"), second, hand_own, rank=t * 10 + 4, loads={("core", 1): 16.0 * width})
        third = ring(2, second)
        return [(t, kind, 2, "own")] + [key + ("share",) for key in third]

    def share_wait(t):
        spans = ((MA, TILES[t][0]), (MB, (TILES[t][1][0], TILES[t][1][1] + TILES[t][2][1])))
        for n, (buf, span) in enumerate(spans):
            if span[1] == 0:
                continue
            copy = pltpu.make_async_remote_copy(
                src_ref=buf.at[core, pl.ds(*span)], dst_ref=buf.at[1 - core, pl.ds(*span)],
                send_sem=s_p.at[t, n], recv_sem=r_p.at[t, n], device_id=partner, device_id_type=MESH,
            )
            copy.wait_send()
            copy.wait_recv()

    def absorb(t, gs):
        for g in gs:
            gx, gy = g // 2, g % 2
            o = None
            for h in range(2):
                tiles = []
                for kind in range(3):
                    for u in range(TILES[t][kind][0], sum(TILES[t][kind])):
                        if kind == 0:
                            rows = [MA[h, u, z, gx, gy * 2 + j] for j in range(2) for z in range(8)]
                            tiles.append(jnp.concatenate(rows, axis=0))
                        else:
                            tiles.append(MB[h, u, gx, gy * 2 : gy * 2 + 2].reshape(256, 128))
                part_o = jnp.dot(jnp.concatenate(tiles, axis=1), X[h * 512 : (h + 1) * 512], preferred_element_type=F32)
                o = part_o if o is None else o + part_o
            o = o.reshape(16, 16, 256)
            re = o[:, :8, :128] - o[:, 8:, 128:]
            im = o[:, :8, 128:] + o[:, 8:, :128]
            Y[g * 128 : (g + 1) * 128, :128] = re.reshape(128, 128).astype(BF)
            Y[g * 128 : (g + 1) * 128, 128:] = im.reshape(128, 128).astype(BF)

    def put_next(k, p, block):
        S[pl.ds(p * 1024 + k, 128, stride=8), :] = block

    def enter():
        pl.semaphore_wait(barrier, 19)

    def to_plane():
        tell(plane, line_y)
        tell(square, cuts)

    def prepare_in():
        get_stem.wait()
        Y[:, :128] = stem[0]
        Y[:, 128:] = stem[1]

    def to_cube():
        pl.semaphore_wait(plane, 3)
        tell(cube, line_x)

    def all_in():
        pl.semaphore_wait(cube, 3)

    def prepare_out():
        snd1[...] = S[...].reshape(128, 16, 128).astype(BF)
        rcv1[m] = snd1[m]

    def start(t):
        if t == 0:
            exchange_wait(snd1, rcv1, 0)
            got = rcv1[...].astype(F32)
            X[:, :128] = got[:, :8, :].reshape(1024, 128).astype(BF)
            X[:, 128:] = got[:, 8:, :].reshape(1024, 128).astype(BF)
        else:
            X[:, :128] = S[:1024].astype(BF)
            X[:, 128:] = S[1024:].astype(BF)
        share_wait(t)

    pairs = ((0, 1), (2, 3), (4, 5), (6, 7))
    enter()
    shares = {}
    for t in range(3):
        shares[t] = []
        for kind in range(3):
            if TILES[t][kind][1] > 0:
                shares[t] += gather_item(t, kind)
    add("plane", [], to_plane, rank=1, start=0.5)
    add("in", [], prepare_in, rank=2, cost=0.3, start=0.6)
    last = ["in"]
    for n, ks in enumerate(pairs):
        add(("p", 0, n), last, functools.partial(permute, 0, put_send, ks), rank=2, cost=0.7)
        last = [("p", 0, n)]
    add("out", last, prepare_out, rank=2, cost=0.4)
    add("cube", ["plane"], to_cube, rank=2, start=3.5)
    add("all", ["cube"], all_in, rank=3, start=6.0)
    last = ["all", "out"]
    for n in range(8):
        lo, hi = max(1, n * 16), (n + 1) * 16
        add(("x", n), last, functools.partial(exchange, snd1, rcv1, 0, lo, hi), cost=0.6, rank=3,
            loads={(d, w): {"x": 40, "y": 64, "z": 80}[d] for d in "xyz" for w in (1, -1)}, start=6.0 + 0.8 * n)
    for n in range(4):
        add(("t", 1, n), [], functools.partial(make_pt, 1, pairs[n]), rank=50, cost=0.3, start=7.0)
        add(("t", 2, n), [], functools.partial(make_pt, 2, pairs[n]), rank=51, cost=0.3, start=7.0)
        add(("t", 3, n), [], functools.partial(make_rt, pairs[n]), rank=52, cost=0.4, start=7.0)
    ready = [("x", n) for n in range(8)]
    for t in range(3):
        add(("s", t), shares[t] + ready, functools.partial(start, t), cost=1.0, rank=30, start=0.0)
        last = [("s", t)]
        for n, gs in enumerate(pairs):
            add(("m", t, n), last, functools.partial(absorb, t, gs), cost=0.5, rank=30)
            last = [("m", t, n)]
        if t < 2:
            for n, ks in enumerate(pairs):
                add(("p", t + 1, n), last + [("t", t + 1, n)], functools.partial(permute, t + 1, put_next, ks), cost=0.5, rank=30)
                last = [("p", t + 1, n)]
        ready = last
    ordered = plan(tasks)
    for task in ordered:
        fns[task["key"]]()

    for p in range(2):
        for j in range(8):
            block = Y[j * 128 : (j + 1) * 128, p * 128 : (p + 1) * 128].astype(F32).T
            S[pl.ds(p * 8 + j, 128, stride=16), :] = block
            Y3T[p * 128 : (p + 1) * 128, j * 128 : (j + 1) * 128] = block.astype(BF)
    snd2[...] = S[...].reshape(128, 16, 128).astype(BF)
    exchange(snd2, rcv2, 1, 1, 64)
    rcv2[m] = snd2[m]

    place = lax.broadcasted_iota(jnp.int32, (128, 256), 0)
    for q in range(8):
        cols = cb[:, q * 256 : (q + 1) * 256]
        got = jnp.dot(Y3T[...], RT[q], preferred_element_type=F32)
        here = (place == cols // 128) & (cols % 128 == m)
        for p in range(2):
            val = jnp.sum(jnp.where(here, got[p * 128 : (p + 1) * 128], 0.0), axis=0, keepdims=True)
            a0[q * 2, p : p + 1, :] = val[:, :128]
            a0[q * 2 + 1, p : p + 1, :] = val[:, 128:]

    def spread(src_of, buf, peers, n):
        copies = []
        for k, peer in enumerate(peers):
            copy = pltpu.make_async_remote_copy(
                src_ref=src_of(k), dst_ref=buf.at[k + 1], send_sem=s_am.at[n, k], recv_sem=r_am.at[n, k],
                device_id=peer, device_id_type=MESH,
            )
            copy.start()
            copies.append(copy)
        return copies

    def collect(buf, copies, mine):
        total = mine
        for copy in copies:
            copy.wait()
        for k in range(len(copies)):
            total = total + buf[k + 1]
        return total

    pl.semaphore_wait(square, 3)
    face = [((c + i) % 4, (me["x"] + j) % 4) for i in range(4) for j in range(4) if i + j > 0]
    sheet = [((me["y"] + i) % 4, (me["z"] + j) % 8) for i in range(4) for j in range(8) if i + j > 0]
    one = spread(lambda k: a0.at[face[k][0] * 4 + face[k][1]], a1, [(i, mode_of(j, me["y"], me["z"])) for i, j in face], 0)
    exchange(snd2, rcv2, 1, 64, 128)
    a2[...] = collect(a1, one, a0[c * 4 + me["x"]])
    two = spread(lambda k: a2, a3, [(c, mode_of(me["x"], i, j)) for i, j in sheet], 1)
    for copy in sent:
        copy.wait_send()
    amp[...] = collect(a3, two, a2[...])

    exchange_wait(snd2, rcv2, 1)
    S[...] = rcv2[...].astype(F32).reshape(2048, 128)
    for p in range(2):
        for j in range(8):
            block = S[pl.ds(p * 8 + j, 128, stride=16), :]
            out[p, j * 128 : (j + 1) * 128, :] = block.T.astype(BF)


def body(stem, branches, order, swap_order, row_bits, column_bits):
    vmem = pl.BlockSpec(memory_space=pltpu.VMEM)
    br = branches.transpose(0, 1, 3, 2).reshape(3, 16, 1024)
    idx = swap_order.reshape(3, 128, 8)
    dma = pltpu.SemaphoreType.DMA
    field, amps = pl.pallas_call(
        kernel,
        out_shape=(jax.ShapeDtypeStruct((2, 1024, 128), BF), jax.ShapeDtypeStruct((2, 128), F32)),
        in_specs=[pl.BlockSpec(memory_space=pltpu.SMEM)] + [pl.BlockSpec(memory_space=pltpu.HBM)] * 2 + [vmem] * 3,
        out_specs=(vmem, vmem),
        scratch_shapes=[
            pltpu.VMEM((2, 1024, 128), BF),
            pltpu.VMEM((3, 16, 1024), BF),
            pltpu.VMEM((2, 3, 8, 4, 4, 16, 128), BF),
            pltpu.VMEM((2, 9, 4, 4, 8, 16, 128), BF),
            pltpu.VMEM((2, 1024, 1024), BF),
            pltpu.VMEM((8, 1024, 256), BF),
            pltpu.VMEM((1024, 256), BF),
            pltpu.VMEM((1024, 256), BF),
            pltpu.VMEM((2048, 128), F32),
            pltpu.VMEM((256, 1024), BF),
            pltpu.VMEM((128, 16, 128), BF),
            pltpu.VMEM((128, 16, 128), BF),
            pltpu.VMEM((128, 16, 128), BF),
            pltpu.VMEM((128, 16, 128), BF),
            pltpu.VMEM((16, 2, 128), F32),
            pltpu.VMEM((16, 2, 128), F32),
            pltpu.VMEM((2, 128), F32),
            pltpu.VMEM((32, 2, 128), F32),
            dma((2,)), dma((2,)),
            dma((9, 12)), dma((9, 12)),
            dma((3, 2)), dma((3, 2)),
            dma((2, 31)), dma((2, 31)),
            dma((2,)),
            pltpu.SemaphoreType.REGULAR, pltpu.SemaphoreType.REGULAR, pltpu.SemaphoreType.REGULAR,
        ],
        compiler_params=pltpu.CompilerParams(collective_id=0, has_side_effects=True, vmem_limit_bytes=48_000_000),
    )(order, stem[0], br, idx, row_bits.reshape(1, 2048), column_bits.reshape(1, 2048))
    m = lax.axis_index("mode")
    amps = lax.dynamic_slice_in_dim(amps, (m % 32) * 4, 4, 1)
    return field[None], amps


def solution(mesh):
    placed = (P("cuts", None, None, "mode"), P(None, None, None, "mode"), P(), P(), P(), P())
    return jax.shard_map(
        body,
        mesh=mesh,
        in_specs=placed,
        out_specs=(P("cuts", None, None, "mode"), P(None, ("cuts", "mode"))),
        check_vma=False,
    )
```
